32 devices in a mesh: leaf: 16 (over z, y, x), sub: 2 (over core).
Axes of the slice: x: 2, y: 2, z: 4, core: 2. Of those that a mesh axis runs over, the one named last changes fastest.
Arguments:
- right_sides: float32 [2, 4, 16, 1536], P(None, None, None, ('leaf', 'sub')), may hold values from -6 to 6
- diag_inverse: float32 [2, 1536, 2880], P(None, ('leaf', 'sub'))
- coupling: float32 [2, 1536, 1344], P(None, ('leaf', 'sub'))
- boundary: int32 [32, 1344], P(('leaf', 'sub')), may hold values from 0 to 2687, as said below
- plane_map: int32 [32, 192], P(('leaf', 'sub')), may hold values from 0 to 191, each once within a row
Outputs:
- plane_field: float32 [2, 16, 6144], P(None, None, ('leaf', 'sub'))
The draws below stay inside these ranges and needn't reach their ends.
Inputs may be any that keep to these rules, and one draw needn't show every extreme that they name: `boundary`: for level l >= 1 (columns e_l .. e_l + n_l - 1 of a row), entries lie in 0 .. (sum of n_a over a < l) - 1 and are equal on all devices d with the same d div (32 / 2^l); the first entry of each such segment is its largest allowed value and the second is 0.
All inputs are finite; a program needn't handle non-finite values.
Results may differ from the reference program's by a relative error of at most 0.0001.
Values sent between devices are 32-bit elements; how exact they have to be, the bound alone decides.
No kernel may reach another device: no remote copies, remote signals or barrier semaphores. Data moves between devices by JAX's collectives and lax.ppermute only.
A program may use at most 64 MiB of HBM per device.

```python
import jax
import jax.numpy as jnp
from jax import lax

SEP_ROWS = 48
SOURCES = 16
LEVELS = 4
ROOT_ORDER = 1536
LOCAL_ROWS = 192
SLOTS = 12
N_LEAF = 16
N_SUB = 2
DEVICES = 32


def column_scales(first_level, factor):
    total_cols = sum((ROOT_ORDER // 2 ** level_index for level_index in range(first_level, LEVELS)))
    columns = jnp.arange(total_cols)
    scales = jnp.zeros((total_cols,), jnp.float32)
    offset = 0
    for level_index in range(first_level, LEVELS):
        front_order = ROOT_ORDER // 2 ** level_index
        inside = (columns >= offset) & (columns < offset + front_order)
        scales = jnp.where(inside, factor / jnp.sqrt(2.0 * front_order), scales)
        offset += front_order
    return (scales, total_cols)


def dense_draw(key, first_level, factor):
    scales, total_cols = column_scales(first_level, factor)
    values = jax.random.normal(key, (2, ROOT_ORDER, total_cols), jnp.float32)
    return values * scales[None, None, :]


def draw_diag_inverse(key, part):
    return dense_draw(jax.random.fold_in(key, 11), 0, 1.0)


def draw_coupling(key, part):
    return dense_draw(jax.random.fold_in(key, 23), 1, 0.6)


def draw_boundary(key, part):
    segments = []
    for level_index in range(1, LEVELS):
        nodes = 2 ** level_index
        front_order = ROOT_ORDER // nodes
        ancestry_len = sum((ROOT_ORDER // 2 ** upper for upper in range(level_index)))
        level_key = jax.random.fold_in(jax.random.fold_in(key, 37), level_index)
        indices = jax.random.randint(level_key, (nodes, front_order), 0, ancestry_len, jnp.int32)
        indices = indices.at[:, 0].set(ancestry_len - 1)
        indices = indices.at[:, 1].set(0)
        segments.append(jnp.repeat(indices, DEVICES // nodes, axis=0))
    return jnp.concatenate(segments, axis=1).astype(jnp.int32)


def block_levels(key, shape, cuts, smallest, high):
    level, own = 1.0, jax.random.fold_in(key, 6)
    for axis_at, blocks in cuts:
        steps = jnp.exp(jax.random.uniform(jax.random.fold_in(own, axis_at), (blocks,), jnp.float32, smallest / len(cuts), high / len(cuts)))
        level = level * jnp.repeat(steps, shape[axis_at] // blocks).reshape([-1 if axis == axis_at else 1 for axis in range(len(shape))])
    return level


def centred(key, dims, spread, limit, cuts=(), dtype=jnp.bfloat16):
    array = spread * jax.random.normal(key, dims, jnp.float32)
    if cuts:
        array = array * block_levels(key, dims, cuts, -0.22, 0.18)
    return jnp.clip(array, -limit, limit).astype(dtype)


def setup_inputs(seed: int = 0) -> dict:
    keys = jax.random.split(jax.random.key(seed), 6)
    return {
        "right_sides": centred(keys[0], (2, LEVELS, SOURCES, ROOT_ORDER), 1.0, 6.0, ((3, 32),), jnp.float32),
        "diag_inverse": draw_diag_inverse(jax.random.fold_in(keys[5], 71), 0),
        "coupling": draw_coupling(jax.random.fold_in(keys[5], 71), 0),
        "boundary": draw_boundary(jax.random.fold_in(keys[5], 71), 0),
        "plane_map": jax.vmap(lambda own: jax.random.permutation(own, LOCAL_ROWS))(jax.random.split(keys[4], DEVICES)).reshape((DEVICES, LOCAL_ROWS)).astype(jnp.int32),
    }


def complex_product(matrix, vectors):
    def mult(left, right):
        return jnp.einsum("sc,rc->sr", left, right, precision=lax.Precision.HIGHEST)
    real_part = mult(vectors[0], matrix[0]) - mult(vectors[1], matrix[1])
    imag_part = mult(vectors[0], matrix[1]) + mult(vectors[1], matrix[0])
    return jnp.stack([real_part, imag_part])


def reference(right_sides, diag_inverse, coupling, boundary, plane_map):
    devices_all = N_LEAF * N_SUB
    root_order = SEP_ROWS * devices_all
    solved = []
    diag_offset = 0
    couple_offset = 0
    for level_index in range(LEVELS):
        members = devices_all // 2 ** level_index
        front_order = SEP_ROWS * members
        pieces = []
        for node_index in range(2 ** level_index):
            first_row = node_index * front_order
            current = right_sides[:, level_index, :, first_row:first_row + front_order]
            if level_index > 0:
                parts = []
                for upper in range(level_index):
                    upper_order = root_order // 2 ** upper
                    upper_node = node_index >> (level_index - upper)
                    parts.append(solved[upper][:, :, upper_node * upper_order:(upper_node + 1) * upper_order])
                ancestry = jnp.concatenate(parts, axis=2)
                indices = boundary[node_index * members, couple_offset:couple_offset + front_order].astype(jnp.int32)
                gathered = jnp.take(ancestry, indices, axis=2)
                block = coupling[:, first_row:first_row + front_order, couple_offset:couple_offset + front_order]
                current = current - complex_product(block, gathered)
            block = diag_inverse[:, first_row:first_row + front_order, diag_offset:diag_offset + front_order]
            pieces.append(complex_product(block, current))
        solved.append(jnp.concatenate(pieces, axis=2))
        diag_offset += front_order
        if level_index > 0:
            couple_offset += front_order
    stacked = jnp.stack(solved, axis=1)
    stacked = stacked.reshape(2, LEVELS, SOURCES, devices_all, SEP_ROWS)
    local_rows = jnp.transpose(stacked, (3, 0, 2, 1, 4)).reshape(devices_all, 2, SOURCES, LOCAL_ROWS)
    picked = jnp.take_along_axis(local_rows, plane_map[:, None, None, :].astype(jnp.int32), axis=3)
    picked = picked.reshape(N_LEAF, N_SUB, 2, SOURCES, N_LEAF, SLOTS)
    picked = jnp.transpose(picked, (2, 3, 4, 1, 0, 5))
    return picked.reshape(2, SOURCES, devices_all * LOCAL_ROWS)
```

```python
import functools

import jax
import jax.numpy as jnp
from jax import lax
from jax.experimental import pallas as pl
from jax.experimental.pallas import tpu as pltpu
from jax.sharding import PartitionSpec as P

LEVELS = 4
LANES = 128
AXES = ("leaf", "sub")


def round_up(value, step):
    return -(-value // step) * step


def roll_left(block, shift):
    shift = shift % LANES
    return block if shift == 0 else pltpu.roll(block, LANES - shift, axis=block.ndim - 1)


def roll_right(block, shift):
    return roll_left(block, LANES - shift % LANES)


def lane_of(shape):
    return lax.broadcasted_iota(jnp.int32, shape, len(shape) - 1)


def split(matrix):
    high = matrix.astype(jnp.bfloat16)
    rest = matrix - high.astype(jnp.float32)
    mid = rest.astype(jnp.bfloat16)
    low = (rest - mid.astype(jnp.float32)).astype(jnp.bfloat16)
    return [high, mid, low]


def weights(vectors, width):
    vectors = jnp.where(lane_of(vectors.shape) < width, vectors, 0.0)
    high = vectors.astype(jnp.bfloat16).astype(jnp.float32)
    rest = vectors - high
    mid = rest.astype(jnp.bfloat16).astype(jnp.float32)
    low = rest - mid
    return (high + roll_right(mid, width) + roll_right(low, 2 * width)).astype(jnp.bfloat16)


def product(real, imag, packed, width):
    rows = real.shape[0]
    stacked = jnp.concatenate(split(real) + split(imag), axis=0)
    terms = jnp.dot(stacked, packed, preferred_element_type=jnp.float32)

    def total(first):
        part = terms[first * rows : (first + 1) * rows]
        part = part + terms[(first + 1) * rows : (first + 2) * rows]
        part = part + terms[(first + 2) * rows : (first + 3) * rows]
        return part + roll_left(part, width) + roll_left(part, 2 * width)

    by_real, by_imag = total(0), total(3)
    half = width // 2
    swapped = jnp.where(
        lane_of(by_imag.shape) < half, -roll_left(by_imag, half), roll_right(by_imag, half)
    )
    return by_real + swapped


def side_by_side(blocks, width):
    lane = lane_of(blocks[0].shape)
    packed = jnp.where(lane < width, blocks[0], 0.0)
    for at in range(1, len(blocks)):
        inside = (lane >= at * width) & (lane < (at + 1) * width)
        packed = jnp.where(inside, roll_right(blocks[at], at * width), packed)
    return packed


def gather_rows(source, index, first, count, target):
    step = 8

    def body(turn, carry):
        for inner in range(step):
            row = turn * step + inner
            target[pl.ds(row, 1), :] = source[pl.ds(index[0, first + row], 1), :]
        return carry

    lax.fori_loop(0, count // step, body, 0)


def spread(wires, target, base, local, flips, lanes_flips, rows, width):
    for entry, flip in enumerate(flips):
        for lane_block, lane_flip in enumerate(lanes_flips):
            place = pl.multiple_of(base + (local ^ (flip ^ lane_flip)) * rows, 8)
            target[pl.ds(place, rows), :] = roll_left(wires[entry], lane_block * width)


class Plan:
    def __init__(self, total, leafs, rows, sources):
        self.total, self.leafs, self.rows, self.sources = total, leafs, rows, sources
        self.width = 2 * sources
        self.bits = total.bit_length() - 1
        self.members = [total >> level for level in range(LEVELS)]
        self.order = [members * rows for members in self.members]
        self.group_rows = round_up(-(-rows // (LANES // self.width)), 8)
        self.groups = -(-rows // self.group_rows)
        self.couple_at = [0, 0]
        for level in range(1, LEVELS):
            self.couple_at.append(self.couple_at[-1] + self.order[level])
        self.couple = self.couple_at[LEVELS]
        self.ancestors = [sum(self.order[:level]) for level in range(LEVELS + 1)]
        own = (LEVELS - 1) * sources
        at = self.couple
        self.rhs_at = at if at % LANES + own <= LANES else round_up(at, LANES)
        self.couple_wide = round_up(self.rhs_at + own, LANES)
        self.flips = [0, 2, 4, 6]

    def shared(self, level):
        return [flip for flip in self.flips if flip < self.members[level]]

    def open_bits(self, level):
        bits = range(self.members[level].bit_length() - 1)
        return [bit for bit in bits if (1 << bit) not in (2, 4)]

    def local(self, level):
        position = lax.axis_index("leaf") * (self.total // self.leafs) + lax.axis_index("sub")
        return position & (self.members[level] - 1)


def transposed(block, scratch):
    scratch[...] = jnp.zeros_like(scratch)
    scratch[0 : block.shape[0], 0 : block.shape[1]] = block
    return scratch[...].T


def rhs_kernel(plan, rhs, wire, late, scratch):
    rows, sources = plan.rows, plan.sources
    first = jnp.concatenate([rhs[0, 0], rhs[1, 0]], axis=0)
    first = transposed(first, scratch)
    padded = plan.groups * plan.group_rows
    blocks = [first[at : at + plan.group_rows] for at in range(0, padded, plan.group_rows)]
    packed = side_by_side(blocks, plan.width)
    wire[...] = jnp.broadcast_to(packed[None], wire.shape)
    for part in range(2):
        later = jnp.concatenate([rhs[part, level] for level in range(1, LEVELS)], axis=0)
        late[part] = transposed(later, scratch)[0:rows]


def coupling_kernel(plan, coupling, late, joined):
    whole = plan.couple // LANES * LANES
    tail = plan.couple - whole
    shift = plan.rhs_at % LANES
    for part in range(2):
        joined[part, :, 0:whole] = coupling[part, :, 0:whole]
        joined[part, :, plan.couple_wide - LANES :] = roll_right(late[part], shift)
        if tail:
            joined[part, :, whole : whole + tail] = coupling[part, :, whole : whole + tail]


def rhs_rows(plan, real, imag, level, shift_cols):
    start = plan.rhs_at // LANES * LANES - shift_cols
    offset = plan.rhs_at % LANES + plan.sources * (level - 1)
    re_part = roll_left(real[:, start : start + LANES], offset)
    im_part = roll_left(imag[:, start : start + LANES], offset - plan.sources)
    return jnp.where(lane_of(re_part.shape) < plan.sources, re_part, im_part)


def unpack_all(plan, wires, target):
    g = plan.group_rows
    flat = wires[...].reshape(plan.total * g, LANES)
    for group in range(plan.groups):
        block = roll_left(flat, group * plan.width).reshape(plan.total, g, LANES)
        count = min(g, plan.rows - group * g)
        target[:, group * g : group * g + count, :] = block[:, 0:count]


def pack_all(plan, rows_block, wire):
    g = plan.group_rows
    padded = plan.groups * g
    if padded > plan.rows:
        extra = jnp.zeros((padded - plan.rows, LANES), jnp.float32)
        rows_block = jnp.concatenate([rows_block, extra], axis=0)
    blocks = [rows_block[at : at + g] for at in range(0, padded, g)]
    wire[...] = jnp.broadcast_to(side_by_side(blocks, plan.width)[None], wire.shape)


def top_kernel(plan, wires, diag, wire, vector):
    unpack_all(plan, wires, vector)
    packed = weights(vector[...].reshape(plan.order[0], LANES), plan.width)
    pack_all(plan, product(diag[0], diag[1], packed, plan.width), wire)


def reduce_rows(plan, level, blocks, bounds, packed_first_col, packed):
    out = []
    first = plan.couple_at[level] - packed_first_col
    for real, imag in blocks:
        cols = slice(first, first + plan.order[level])
        value = product(real[:, cols], imag[:, cols], packed, plan.width)
        out.append(rhs_rows(plan, real, imag, level, packed_first_col) - value)
    return out


def first_reduce_kernel(
    plan, wires, index, own, from_x, from_y, diag_re, diag_im, wire, top, rest, bounds
):
    unpack_all(plan, wires, top)
    gather_rows(
        top.reshape(plan.order[0], LANES), index, plan.couple_at[1], plan.order[1], bounds
    )
    blocks = [
        (own.at[0], own.at[1]),
        (from_x.at[0], from_x.at[1]),
        (from_y.at[0], from_y.at[1]),
        (diag_re, diag_im),
    ]
    packed = weights(bounds[...], plan.width)
    wire[...] = side_by_side(reduce_rows(plan, 1, blocks, bounds, 0, packed), plan.width)
    for at, (real, imag) in enumerate(blocks):
        rest[at, 0] = real[:, plan.order[1] :]
        rest[at, 1] = imag[:, plan.order[1] :]


def first_solve_kernel(plan, flips, wires, own, from_x, from_y, diag_re, diag_im, wire, rest, vector):
    order = plan.order[1]
    spread(wires, vector, 0, plan.local(1), flips, plan.shared(1), plan.rows, plan.width)
    packed = weights(vector[...], plan.width)
    blocks = [
        (own.at[0], own.at[1]),
        (from_x.at[0], from_x.at[1]),
        (from_y.at[0], from_y.at[1]),
        (diag_re, diag_im),
    ]
    solved = [product(re[:, 0:order], im[:, 0:order], packed, plan.width) for re, im in blocks]
    wire[...] = side_by_side(solved, plan.width)
    for at, (real, imag) in enumerate(blocks):
        rest[at, 0] = real[:, order:]
        rest[at, 1] = imag[:, order:]


def pack_owners(plan, row_map, local_rows, packing, out):
    slots = plan.rows * LEVELS // plan.leafs
    per_row = LANES // plan.width
    packing[...] = jnp.zeros_like(packing)

    def body(owner, carry):
        for slot in range(slots):
            row = row_map[0, owner * slots + slot]
            packing[slot % per_row, owner, pl.ds(slot // per_row, 1), :] = local_rows[
                pl.ds(row, 1), :
            ]
        return carry

    lax.fori_loop(0, plan.leafs, body, 0)
    lane = lane_of(out.shape)
    total = jnp.where(lane < plan.width, packing[0], 0.0)
    for at in range(1, per_row):
        inside = (lane >= at * plan.width) & (lane < (at + 1) * plan.width)
        total = jnp.where(inside, roll_right(packing[at], at * plan.width), total)
    out[...] = total


def own_rows(plan, vector, level):
    place = pl.multiple_of(plan.ancestors[level] + plan.local(level) * plan.rows, 8)
    return vector[pl.ds(place, plan.rows), :]


def tail_kernel(
    plan, flips, top, wires, index, row_map, couple, couple_far, diag, diag_far, diag_last,
    out, vector, bounds, front, local_rows, packing,
):
    rows, width = plan.rows, plan.width
    vector[0 : plan.order[0], :] = top[...]
    spread(wires, vector, plan.order[0], plan.local(1), flips, plan.shared(1), rows, width)
    cut = plan.order[1]

    def held(level):
        found = []
        for at, flip in enumerate(plan.shared(level)):
            found.append((flip, couple.at[at], diag.at[at]))
            found.append((flip ^ 1, couple_far.at[at], diag_far.at[at]))
        return found

    for level in range(2, LEVELS):
        order = plan.order[level]
        local = plan.local(level)
        gather_rows(vector, index, plan.couple_at[level], order, bounds)
        packed = weights(bounds[0:order, :], width)
        blocks = [(pair.at[0], pair.at[1]) for _, pair, _ in held(level)]
        reduced = reduce_rows(plan, level, blocks, bounds, cut, packed)
        for (flip, _, _), value in zip(held(level), reduced):
            front[pl.ds(pl.multiple_of((local ^ flip) * rows, 8), rows), :] = value
        packed = weights(front[0:order, :], width)
        base = plan.ancestors[level]
        if level + 1 < LEVELS:
            for flip, _, pair in held(level):
                solved = product(pair[0], pair[1], packed, width)
                place = pl.multiple_of(base + (local ^ flip) * rows, 8)
                vector[pl.ds(place, rows), :] = solved
        else:
            local_rows[level * rows :, :] = product(diag_last[0], diag_last[1], packed, width)
    for level in range(LEVELS - 1):
        local_rows[level * rows : (level + 1) * rows, :] = own_rows(plan, vector, level)
    pack_owners(plan, row_map, local_rows, packing, out)


def reduce_kernel(plan, level, flips, top, wires, index, couple, wire, vector, bounds):
    rows, width = plan.rows, plan.width
    vector[0 : plan.ancestors[level - 1], :] = top[...]
    spread(
        wires, vector, plan.ancestors[level - 1], plan.local(level - 1), flips,
        plan.shared(level - 1), rows, width,
    )
    gather_rows(vector, index, plan.couple_at[level], plan.order[level], bounds)
    blocks = [(couple.at[at, 0], couple.at[at, 1]) for at in range(len(plan.shared(level)))]
    packed = weights(bounds[...], width)
    wire[...] = side_by_side(
        reduce_rows(plan, level, blocks, bounds, plan.order[1], packed), width
    )


def solve_kernel(plan, level, flips, first_col, wires, diag, wire, vector):
    spread(wires, vector, 0, plan.local(level), flips, plan.shared(level), plan.rows, plan.width)
    packed = weights(vector[...], plan.width)
    cols = slice(first_col, first_col + plan.order[level])
    solved = [
        product(diag[at, 0, :, cols], diag[at, 1, :, cols], packed, plan.width)
        for at in range(len(plan.shared(level)))
    ]
    wire[...] = side_by_side(solved, plan.width)


def last_kernel(plan, flips, top, wires, row_map, diag_last, out, front, local_rows, packing):
    level = LEVELS - 1
    rows, width = plan.rows, plan.width
    spread(wires, front, 0, plan.local(level), flips, plan.shared(level), rows, width)
    packed = weights(front[...], width)
    local_rows[level * rows :, :] = product(diag_last[0], diag_last[1], packed, width)
    for upper in range(level):
        local_rows[upper * rows : (upper + 1) * rows, :] = own_rows(plan, top, upper)
    pack_owners(plan, row_map, local_rows, packing, out)


def owner_kernel(plan, received, out, scratch):
    slots = plan.rows * LEVELS // plan.leafs
    per_row = LANES // plan.width
    for slot in range(slots):
        block = roll_left(received[:, slot // per_row, :], slot % per_row * plan.width)
        scratch[pl.ds(slot, plan.leafs, stride=slots), :] = block
    out[...] = scratch[...].T[0 : plan.width]


def call(kernel, plan, outs, scratch, args, scalars=(), static=()):
    specs = []
    for at in range(len(args)):
        space = pltpu.SMEM if at in scalars else pltpu.VMEM
        specs.append(pl.BlockSpec(memory_space=space))
    shapes = [jax.ShapeDtypeStruct(shape, jnp.float32) for shape in outs]
    return pl.pallas_call(
        functools.partial(kernel, plan, *static),
        out_shape=shapes,
        in_specs=specs,
        out_specs=[pl.BlockSpec(memory_space=pltpu.VMEM)] * len(outs),
        scratch_shapes=[pltpu.VMEM(shape, jnp.float32) for shape in scratch],
        compiler_params=pltpu.CompilerParams(vmem_limit_bytes=40 << 20),
    )(*args)


def local(right_sides, diag_inverse, coupling, boundary, plane_map):
    total = lax.axis_size(AXES)
    leafs = lax.axis_size("leaf")
    sources, rows = right_sides.shape[2], right_sides.shape[3]
    plan = Plan(total, leafs, rows, sources)
    order = plan.order
    per_row = LANES // plan.width
    owner_rows = -(-(rows * LEVELS // leafs) // per_row)
    packing = (per_row, leafs, owner_rows, LANES)
    wire_shape = (total, plan.group_rows, LANES)
    block = (rows, LANES)

    def hop(array, bit):
        route = [(device, device ^ (1 << bit)) for device in range(total)]
        return lax.ppermute(array, AXES, route)

    def exchange(wire, level):
        current, flips = wire[None], [0]
        for bit in plan.open_bits(level):
            current = jnp.concatenate([current, hop(current, bit)], axis=0)
            flips = flips + [flip ^ (1 << bit) for flip in flips]
        return current, flips

    def to_all(wire):
        return lax.all_to_all(wire, AXES, 0, 0)

    def neighbours(array):
        from_x, from_y = hop(array, 1), hop(array, 2)
        return array, from_x, from_y

    def beyond(pieces):
        own, from_x, from_y = pieces
        return (own, from_x, from_y, hop(from_x[0], 2), hop(from_y[1], 1))

    diag_top = diag_inverse[:, :, : order[0]]
    middle = sum(order[:-1])
    diag_mid = diag_inverse[:, :, order[0] : middle]
    diag_last = diag_inverse[:, :, middle:]

    wire, late = call(
        rhs_kernel, plan, [wire_shape, (2, rows, LANES)], [(LANES, LANES)], [right_sides]
    )
    (joined,) = call(coupling_kernel, plan, [(2, rows, plan.couple_wide)], [], [coupling, late])
    couple = neighbours(joined)
    gathered = to_all(wire)
    couple = beyond(couple)
    diag_mid, gathered = lax.optimization_barrier((diag_mid, gathered))
    diag = neighbours(diag_mid)
    (wire,) = call(
        top_kernel, plan, [wire_shape], [(total, rows, LANES)], [gathered, diag_top]
    )
    gathered = to_all(wire)
    diag = beyond(diag)
    wire, top, couple_rest = call(
        first_reduce_kernel, plan,
        [block, (total, rows, LANES), (4, 2, rows, plan.couple_wide - order[1])],
        [(order[1], LANES)],
        [gathered, boundary, *couple], scalars=(1,),
    )
    top = top.reshape(order[0], LANES)
    wires, flips = exchange(wire, 1)
    wire, diag_rest = call(
        first_solve_kernel, plan, [block, (4, 2, rows, diag_mid.shape[2] - order[1])],
        [(order[1], LANES)], [wires, *diag], static=(flips,),
    )
    wires, flips = exchange(wire, 1)
    if plan.members[2] <= 8:
        couple_far, diag_far = hop(couple_rest, 0), hop(diag_rest, 0)
        (packed,) = call(
            tail_kernel, plan, [(leafs, owner_rows, LANES)],
            [
                (plan.ancestors[LEVELS - 1], LANES), (order[2], LANES), (order[2], LANES),
                (LEVELS * rows, LANES), packing,
            ],
            [
                top, wires, boundary, plane_map, couple_rest, couple_far, diag_rest, diag_far,
                diag_last,
            ],
            scalars=(2, 3), static=(flips,),
        )
    else:
        first_col = 0
        for level in range(2, LEVELS):
            wire, top = call(
                reduce_kernel, plan, [block, (plan.ancestors[level], LANES)],
                [(order[level], LANES)],
                [top, wires, boundary, couple_rest], scalars=(2,), static=(level, flips),
            )
            wires, flips = exchange(wire, level)
            if level + 1 < LEVELS:
                (wire,) = call(
                    solve_kernel, plan, [block], [(order[level], LANES)],
                    [wires, diag_rest], static=(level, flips, first_col),
                )
                first_col += order[level]
                wires, flips = exchange(wire, level)
        (packed,) = call(
            last_kernel, plan, [(leafs, owner_rows, LANES)],
            [(order[-1], LANES), (LEVELS * rows, LANES), packing],
            [top, wires, plane_map, diag_last], scalars=(2,), static=(flips,),
        )
    received = lax.all_to_all(packed, "leaf", 0, 0)
    (field,) = call(
        owner_kernel, plan, [(plan.width, LEVELS * rows)], [(LEVELS * rows, LANES)], [received]
    )
    return field.reshape(2, sources, LEVELS * rows)


def solution(mesh):
    in_specs = (
        P(None, None, None, AXES),
        P(None, AXES, None),
        P(None, AXES, None),
        P(AXES, None),
        P(AXES, None),
    )
    out_specs = P(None, None, AXES)
    return jax.shard_map(local, mesh=mesh, in_specs=in_specs, out_specs=out_specs, check_vma=False)
```

```python
import functools

import jax
import jax.numpy as jnp
from jax import lax
from jax.experimental import pallas as pl
from jax.experimental.pallas import tpu as pltpu
from jax.sharding import PartitionSpec as P


LEVELS = 4
LANES = 128
AXES = ("leaf", "sub")


def round_up(value, step):
    return -(-value // step) * step


def roll_left(block, shift):
    shift = shift % LANES
    return block if shift == 0 else pltpu.roll(block, LANES - shift, axis=block.ndim - 1)


def roll_right(block, shift):
    return roll_left(block, LANES - shift % LANES)


def lane_of(shape):
    return lax.broadcasted_iota(jnp.int32, shape, len(shape) - 1)


def split(matrix):
    high = matrix.astype(jnp.bfloat16)
    rest = matrix - high.astype(jnp.float32)
    mid = rest.astype(jnp.bfloat16)
    low = (rest - mid.astype(jnp.float32)).astype(jnp.bfloat16)
    return [high, mid, low]


def weights(vectors, width):
    vectors = jnp.where(lane_of(vectors.shape) < width, vectors, 0.0)
    high = vectors.astype(jnp.bfloat16).astype(jnp.float32)
    rest = vectors - high
    mid = rest.astype(jnp.bfloat16).astype(jnp.float32)
    low = rest - mid
    return (high + roll_right(mid, width) + roll_right(low, 2 * width)).astype(jnp.bfloat16)


def product(real, imag, packed, width):
    rows = real.shape[0]
    stacked = jnp.concatenate(split(real) + split(imag), axis=0)
    terms = jnp.dot(stacked, packed, preferred_element_type=jnp.float32)

    def total(first):
        part = terms[first * rows : (first + 1) * rows]
        part = part + terms[(first + 1) * rows : (first + 2) * rows]
        part = part + terms[(first + 2) * rows : (first + 3) * rows]
        return part + roll_left(part, width) + roll_left(part, 2 * width)

    by_real, by_imag = total(0), total(3)
    half = width // 2
    swapped = jnp.where(
        lane_of(by_imag.shape) < half, -roll_left(by_imag, half), roll_right(by_imag, half)
    )
    return by_real + swapped


def side_by_side(blocks, width):
    lane = lane_of(blocks[0].shape)
    packed = jnp.where(lane < width, blocks[0], 0.0)
    for at in range(1, len(blocks)):
        inside = (lane >= at * width) & (lane < (at + 1) * width)
        packed = jnp.where(inside, roll_right(blocks[at], at * width), packed)
    return packed


def gather_rows(source, index, first, count, target):
    step = 8

    def body(turn, carry):
        for inner in range(step):
            row = turn * step + inner
            target[pl.ds(row, 1), :] = source[pl.ds(index[0, first + row], 1), :]
        return carry

    lax.fori_loop(0, count // step, body, 0)


def spread(wires, target, base, local, flips, lanes_flips, rows, width):
    for entry, flip in enumerate(flips):
        for lane_block, lane_flip in enumerate(lanes_flips):
            place = pl.multiple_of(base + (local ^ (flip ^ lane_flip)) * rows, 8)
            target[pl.ds(place, rows), :] = roll_left(wires[entry], lane_block * width)


class Plan:
    def __init__(self, total, leafs, rows, sources):
        self.total, self.leafs, self.rows, self.sources = total, leafs, rows, sources
        self.width = 2 * sources
        self.members = [total >> level for level in range(LEVELS)]
        self.order = [members * rows for members in self.members]
        self.group_rows = round_up(-(-rows // (LANES // self.width)), 8)
        self.groups = -(-rows // self.group_rows)
        self.couple_at = [0, 0]
        for level in range(1, LEVELS):
            self.couple_at.append(self.couple_at[-1] + self.order[level])
        self.couple = self.couple_at[LEVELS]
        self.ancestors = [sum(self.order[:level]) for level in range(LEVELS + 1)]
        own = (LEVELS - 1) * sources
        at = self.couple
        self.rhs_at = at if at % LANES + own <= LANES else round_up(at, LANES)
        self.couple_wide = round_up(self.rhs_at + own, LANES)
        self.flips = [0, 2, 4, 6]

    def shared(self, level):
        return [flip for flip in self.flips if flip < self.members[level]]

    def open_bits(self, level):
        bits = range(self.members[level].bit_length() - 1)
        return [bit for bit in bits if (1 << bit) not in (2, 4)]

    def local(self, level):
        position = lax.axis_index("leaf") * (self.total // self.leafs) + lax.axis_index("sub")
        return position & (self.members[level] - 1)


def transposed(block, scratch):
    scratch[...] = jnp.zeros_like(scratch)
    scratch[0 : block.shape[0], 0 : block.shape[1]] = block
    return scratch[...].T


def rhs_kernel(plan, rhs, wire, late, scratch):
    rows = plan.rows
    first = jnp.concatenate([rhs[0, 0], rhs[1, 0]], axis=0)
    first = transposed(first, scratch)
    padded = plan.groups * plan.group_rows
    blocks = [first[at : at + plan.group_rows] for at in range(0, padded, plan.group_rows)]
    packed = side_by_side(blocks, plan.width)
    wire[...] = jnp.broadcast_to(packed[None], wire.shape)
    for part in range(2):
        later = jnp.concatenate([rhs[part, level] for level in range(1, LEVELS)], axis=0)
        late[part] = transposed(later, scratch)[0:rows]


def coupling_kernel(plan, coupling, late, joined):
    whole = plan.couple // LANES * LANES
    tail = plan.couple - whole
    shift = plan.rhs_at % LANES
    for part in range(2):
        joined[part, :, 0:whole] = coupling[part, :, 0:whole]
        joined[part, :, plan.couple_wide - LANES :] = roll_right(late[part], shift)
        if tail:
            joined[part, :, whole : whole + tail] = coupling[part, :, whole : whole + tail]


def rhs_rows(plan, real, imag, level, shift_cols):
    start = plan.rhs_at // LANES * LANES - shift_cols
    offset = plan.rhs_at % LANES + plan.sources * (level - 1)
    re_part = roll_left(real[:, start : start + LANES], offset)
    im_part = roll_left(imag[:, start : start + LANES], offset - plan.sources)
    return jnp.where(lane_of(re_part.shape) < plan.sources, re_part, im_part)


def unpack_all(plan, near, far, target):
    g = plan.group_rows
    core = lax.axis_index("sub")
    for place, wires in ((core, near), (core ^ 1, far)):
        flat = wires[...].reshape(plan.leafs * g, LANES)
        for group in range(plan.groups):
            block = roll_left(flat, group * plan.width).reshape(plan.leafs, g, LANES)
            count = min(g, plan.rows - group * g)
            target[:, place, group * g : group * g + count, :] = block[:, 0:count]


def pack_all(plan, rows_block, wire):
    g = plan.group_rows
    padded = plan.groups * g
    if padded > plan.rows:
        extra = jnp.zeros((padded - plan.rows, LANES), jnp.float32)
        rows_block = jnp.concatenate([rows_block, extra], axis=0)
    blocks = [rows_block[at : at + g] for at in range(0, padded, g)]
    wire[...] = jnp.broadcast_to(side_by_side(blocks, plan.width)[None], wire.shape)


def top_kernel(plan, near, far, diag, wire, vector):
    unpack_all(plan, near, far, vector)
    packed = weights(vector[...].reshape(plan.order[0], LANES), plan.width)
    pack_all(plan, product(diag[0], diag[1], packed, plan.width), wire)


def reduce_rows(plan, level, blocks, packed_first_col, packed):
    out = []
    first = plan.couple_at[level] - packed_first_col
    for real, imag in blocks:
        cols = slice(first, first + plan.order[level])
        value = product(real[:, cols], imag[:, cols], packed, plan.width)
        out.append(rhs_rows(plan, real, imag, level, packed_first_col) - value)
    return out


def first_reduce_kernel(
    plan, near, far, index, own, from_x, from_y, diag_re, diag_im, wire, top, rest, bounds
):
    unpack_all(plan, near, far, top)
    gather_rows(
        top.reshape(plan.order[0], LANES), index, plan.couple_at[1], plan.order[1], bounds
    )
    blocks = [
        (own.at[0], own.at[1]),
        (from_x.at[0], from_x.at[1]),
        (from_y.at[0], from_y.at[1]),
        (diag_re, diag_im),
    ]
    packed = weights(bounds[...], plan.width)
    wire[...] = side_by_side(reduce_rows(plan, 1, blocks, 0, packed), plan.width)
    for at, (real, imag) in enumerate(blocks):
        rest[at, 0] = real[:, plan.order[1] :]
        rest[at, 1] = imag[:, plan.order[1] :]


def first_solve_kernel(plan, flips, wires, own, from_x, from_y, diag_re, diag_im, wire, rest, vector):
    order = plan.order[1]
    spread(wires, vector, 0, plan.local(1), flips, plan.shared(1), plan.rows, plan.width)
    packed = weights(vector[...], plan.width)
    blocks = [
        (own.at[0], own.at[1]),
        (from_x.at[0], from_x.at[1]),
        (from_y.at[0], from_y.at[1]),
        (diag_re, diag_im),
    ]
    solved = [product(re[:, 0:order], im[:, 0:order], packed, plan.width) for re, im in blocks]
    wire[...] = side_by_side(solved, plan.width)
    for at, (real, imag) in enumerate(blocks):
        rest[at, 0] = real[:, order:]
        rest[at, 1] = imag[:, order:]


def pack_owners(plan, row_map, local_rows, packing, out):
    slots = plan.rows * LEVELS // plan.leafs
    per_row = LANES // plan.width
    packing[...] = jnp.zeros_like(packing)

    def body(owner, carry):
        for slot in range(slots):
            row = row_map[0, owner * slots + slot]
            packing[slot % per_row, owner, pl.ds(slot // per_row, 1), :] = local_rows[
                pl.ds(row, 1), :
            ]
        return carry

    lax.fori_loop(0, plan.leafs, body, 0)
    lane = lane_of(out.shape)
    total = jnp.where(lane < plan.width, packing[0], 0.0)
    for at in range(1, per_row):
        inside = (lane >= at * plan.width) & (lane < (at + 1) * plan.width)
        total = jnp.where(inside, roll_right(packing[at], at * plan.width), total)
    out[...] = total


def own_rows(plan, vector, level):
    place = pl.multiple_of(plan.ancestors[level] + plan.local(level) * plan.rows, 8)
    return vector[pl.ds(place, plan.rows), :]


def tail_kernel(
    plan, flips, top, wires, index, row_map, couple, couple_far, diag, diag_far, diag_last,
    out, vector, bounds, front, local_rows, packing,
):
    rows, width = plan.rows, plan.width
    vector[0 : plan.order[0], :] = top[...]
    spread(wires, vector, plan.order[0], plan.local(1), flips, plan.shared(1), rows, width)
    cut = plan.order[1]

    def held(level):
        found = []
        for at, flip in enumerate(plan.shared(level)):
            found.append((flip, couple.at[at], diag.at[at]))
            found.append((flip ^ 1, couple_far.at[at], diag_far.at[at]))
        return found

    for level in range(2, LEVELS):
        order = plan.order[level]
        local = plan.local(level)
        gather_rows(vector, index, plan.couple_at[level], order, bounds)
        packed = weights(bounds[0:order, :], width)
        blocks = [(pair.at[0], pair.at[1]) for _, pair, _ in held(level)]
        reduced = reduce_rows(plan, level, blocks, cut, packed)
        for (flip, _, _), value in zip(held(level), reduced):
            front[pl.ds(pl.multiple_of((local ^ flip) * rows, 8), rows), :] = value
        packed = weights(front[0:order, :], width)
        base = plan.ancestors[level]
        if level + 1 < LEVELS:
            for flip, _, pair in held(level):
                solved = product(pair[0], pair[1], packed, width)
                place = pl.multiple_of(base + (local ^ flip) * rows, 8)
                vector[pl.ds(place, rows), :] = solved
        else:
            local_rows[level * rows :, :] = product(diag_last[0], diag_last[1], packed, width)
    for level in range(LEVELS - 1):
        local_rows[level * rows : (level + 1) * rows, :] = own_rows(plan, vector, level)
    pack_owners(plan, row_map, local_rows, packing, out)


def reduce_kernel(plan, level, flips, top, wires, index, couple, wire, vector, bounds):
    rows, width = plan.rows, plan.width
    vector[0 : plan.ancestors[level - 1], :] = top[...]
    spread(
        wires, vector, plan.ancestors[level - 1], plan.local(level - 1), flips,
        plan.shared(level - 1), rows, width,
    )
    gather_rows(vector, index, plan.couple_at[level], plan.order[level], bounds)
    blocks = [(couple.at[at, 0], couple.at[at, 1]) for at in range(len(plan.shared(level)))]
    packed = weights(bounds[...], width)
    wire[...] = side_by_side(reduce_rows(plan, level, blocks, plan.order[1], packed), width)


def solve_kernel(plan, level, flips, first_col, wires, diag, wire, vector):
    spread(wires, vector, 0, plan.local(level), flips, plan.shared(level), plan.rows, plan.width)
    packed = weights(vector[...], plan.width)
    cols = slice(first_col, first_col + plan.order[level])
    solved = [
        product(diag[at, 0, :, cols], diag[at, 1, :, cols], packed, plan.width)
        for at in range(len(plan.shared(level)))
    ]
    wire[...] = side_by_side(solved, plan.width)


def last_kernel(plan, flips, top, wires, row_map, diag_last, out, front, local_rows, packing):
    level = LEVELS - 1
    rows, width = plan.rows, plan.width
    spread(wires, front, 0, plan.local(level), flips, plan.shared(level), rows, width)
    packed = weights(front[...], width)
    local_rows[level * rows :, :] = product(diag_last[0], diag_last[1], packed, width)
    for upper in range(level):
        local_rows[upper * rows : (upper + 1) * rows, :] = own_rows(plan, top, upper)
    pack_owners(plan, row_map, local_rows, packing, out)


def owner_kernel(plan, received, out, scratch):
    slots = plan.rows * LEVELS // plan.leafs
    per_row = LANES // plan.width
    for slot in range(slots):
        block = roll_left(received[:, slot // per_row, :], slot % per_row * plan.width)
        scratch[pl.ds(slot, plan.leafs, stride=slots), :] = block
    out[...] = scratch[...].T[0 : plan.width]


def call(kernel, plan, outs, scratch, args, scalars=(), static=()):
    specs = []
    for at in range(len(args)):
        space = pltpu.SMEM if at in scalars else pltpu.VMEM
        specs.append(pl.BlockSpec(memory_space=space))
    shapes = [jax.ShapeDtypeStruct(shape, jnp.float32) for shape in outs]
    return pl.pallas_call(
        functools.partial(kernel, plan, *static),
        out_shape=shapes,
        in_specs=specs,
        out_specs=[pl.BlockSpec(memory_space=pltpu.VMEM)] * len(outs),
        scratch_shapes=[pltpu.VMEM(shape, jnp.float32) for shape in scratch],
        compiler_params=pltpu.CompilerParams(vmem_limit_bytes=16 << 20),
    )(*args)


def local(right_sides, diag_inverse, coupling, boundary, plane_map):
    total = lax.axis_size(AXES)
    leafs = lax.axis_size("leaf")
    sources, rows = right_sides.shape[2], right_sides.shape[3]
    plan = Plan(total, leafs, rows, sources)
    order = plan.order
    per_row = LANES // plan.width
    owner_rows = -(-(rows * LEVELS // leafs) // per_row)
    packing = (per_row, leafs, owner_rows, LANES)
    wire_shape = (leafs, plan.group_rows, LANES)
    whole_shape = (leafs, total // leafs, rows, LANES)
    block = (rows, LANES)

    def hop(array, bit):
        route = [(device, device ^ (1 << bit)) for device in range(total)]
        return lax.ppermute(array, AXES, route)

    def exchange(wire, level):
        current, flips = wire[None], [0]
        for bit in plan.open_bits(level):
            found = hop(current, bit)
            current = jnp.concatenate([current, found], axis=0)
            flips = flips + [flip ^ (1 << bit) for flip in flips]
        return current, flips

    def to_all(wire):
        near = lax.all_to_all(wire, "leaf", 0, 0)
        return near, hop(near, 0)

    def neighbours(array):
        return array, hop(array, 1), hop(array, 2)

    def beyond(pieces):
        own, from_x, from_y = pieces
        real = hop(from_x[0], 2)
        return (own, from_x, from_y, real, hop(from_y[1], 1))

    diag_top = diag_inverse[:, :, : order[0]]
    middle = sum(order[:-1])
    diag_mid = diag_inverse[:, :, order[0] : middle]
    diag_last = diag_inverse[:, :, middle:]

    wire, late = call(
        rhs_kernel, plan, [wire_shape, (2, rows, LANES)], [(LANES, LANES)], [right_sides]
    )
    (joined,) = call(coupling_kernel, plan, [(2, rows, plan.couple_wide)], [], [coupling, late])
    gathered = to_all(wire)
    couple = beyond(neighbours(joined))
    (wire,) = call(top_kernel, plan, [wire_shape], [whole_shape], [*gathered, diag_top])
    gathered = to_all(wire)
    diag = beyond(neighbours(diag_mid))
    wire, top, couple_rest = call(
        first_reduce_kernel, plan,
        [block, whole_shape, (4, 2, rows, plan.couple_wide - order[1])],
        [(order[1], LANES)],
        [*gathered, boundary, *couple], scalars=(2,),
    )
    top = top.reshape(order[0], LANES)
    wires, flips = exchange(wire, 1)
    wire, diag_rest = call(
        first_solve_kernel, plan, [block, (4, 2, rows, diag_mid.shape[2] - order[1])],
        [(order[1], LANES)], [wires, *diag], static=(flips,),
    )
    wires, flips = exchange(wire, 1)
    if plan.members[2] <= 8:
        couple_far = hop(couple_rest, 0)
        diag_far = hop(diag_rest, 0)
        (packed,) = call(
            tail_kernel, plan, [(leafs, owner_rows, LANES)],
            [
                (plan.ancestors[LEVELS - 1], LANES), (order[2], LANES), (order[2], LANES),
                (LEVELS * rows, LANES), packing,
            ],
            [
                top, wires, boundary, plane_map, couple_rest, couple_far, diag_rest, diag_far,
                diag_last,
            ],
            scalars=(2, 3), static=(flips,),
        )
    else:
        first_col = 0
        for level in range(2, LEVELS):
            wire, top = call(
                reduce_kernel, plan, [block, (plan.ancestors[level], LANES)],
                [(order[level], LANES)],
                [top, wires, boundary, couple_rest], scalars=(2,), static=(level, flips),
            )
            wires, flips = exchange(wire, level)
            if level + 1 < LEVELS:
                (wire,) = call(
                    solve_kernel, plan, [block], [(order[level], LANES)],
                    [wires, diag_rest], static=(level, flips, first_col),
                )
                first_col += order[level]
                wires, flips = exchange(wire, level)
        (packed,) = call(
            last_kernel, plan, [(leafs, owner_rows, LANES)],
            [(order[-1], LANES), (LEVELS * rows, LANES), packing],
            [top, wires, plane_map, diag_last], scalars=(2,), static=(flips,),
        )
    received = lax.all_to_all(packed, "leaf", 0, 0)
    (field,) = call(
        owner_kernel, plan, [(plan.width, LEVELS * rows)], [(LEVELS * rows, LANES)], [received]
    )
    return field.reshape(2, sources, LEVELS * rows)


def solution(mesh):
    in_specs = (
        P(None, None, None, AXES),
        P(None, AXES, None),
        P(None, AXES, None),
        P(AXES, None),
        P(AXES, None),
    )
    out_specs = P(None, None, AXES)
    return jax.shard_map(local, mesh=mesh, in_specs=in_specs, out_specs=out_specs, check_vma=False)
```

```python
import functools

import jax
import jax.numpy as jnp
from jax import lax
from jax.experimental import pallas as pl
from jax.experimental.pallas import tpu as pltpu
from jax.sharding import PartitionSpec as P


LEVELS = 4
LANES = 128
AXES = ("leaf", "sub")


def round_up(value, step):
    return -(-value // step) * step


def roll_left(block, shift):
    shift = shift % LANES
    return block if shift == 0 else pltpu.roll(block, LANES - shift, axis=block.ndim - 1)


def roll_right(block, shift):
    return roll_left(block, LANES - shift % LANES)


def lane_of(shape):
    return lax.broadcasted_iota(jnp.int32, shape, len(shape) - 1)


def split(matrix):
    high = matrix.astype(jnp.bfloat16)
    rest = matrix - high.astype(jnp.float32)
    mid = rest.astype(jnp.bfloat16)
    low = (rest - mid.astype(jnp.float32)).astype(jnp.bfloat16)
    return [high, mid, low]


def weights(vectors, width):
    vectors = jnp.where(lane_of(vectors.shape) < width, vectors, 0.0)
    high = vectors.astype(jnp.bfloat16).astype(jnp.float32)
    rest = vectors - high
    mid = rest.astype(jnp.bfloat16).astype(jnp.float32)
    low = rest - mid
    return (high + roll_right(mid, width) + roll_right(low, 2 * width)).astype(jnp.bfloat16)


def product(real, imag, packed, width):
    rows = real.shape[0]
    stacked = jnp.concatenate(split(real) + split(imag), axis=0)
    terms = jnp.dot(stacked, packed, preferred_element_type=jnp.float32)

    def total(first):
        part = terms[first * rows : (first + 1) * rows]
        part = part + terms[(first + 1) * rows : (first + 2) * rows]
        part = part + terms[(first + 2) * rows : (first + 3) * rows]
        return part + roll_left(part, width) + roll_left(part, 2 * width)

    by_real, by_imag = total(0), total(3)
    half = width // 2
    swapped = jnp.where(
        lane_of(by_imag.shape) < half, -roll_left(by_imag, half), roll_right(by_imag, half)
    )
    return by_real + swapped


def side_by_side(blocks, width):
    lane = lane_of(blocks[0].shape)
    packed = jnp.where(lane < width, blocks[0], 0.0)
    for at in range(1, len(blocks)):
        inside = (lane >= at * width) & (lane < (at + 1) * width)
        packed = jnp.where(inside, roll_right(blocks[at], at * width), packed)
    return packed


def gather_rows(source, index, first, count, target):
    step = 8

    def body(turn, carry):
        for inner in range(step):
            row = turn * step + inner
            target[pl.ds(row, 1), :] = source[pl.ds(index[0, first + row], 1), :]
        return carry

    lax.fori_loop(0, count // step, body, 0)


def spread(wires, target, base, local, flips, lanes_flips, rows, width):
    for entry, flip in enumerate(flips):
        wire = wires[entry][...]
        for lane_block, lane_flip in enumerate(lanes_flips):
            place = pl.multiple_of(base + (local ^ (flip ^ lane_flip)) * rows, 8)
            target[pl.ds(place, rows), :] = roll_left(wire, lane_block * width)


class Plan:
    def __init__(self, total, leafs, rows, sources):
        self.total, self.leafs, self.rows, self.sources = total, leafs, rows, sources
        self.width = 2 * sources
        self.members = [total >> level for level in range(LEVELS)]
        self.order = [members * rows for members in self.members]
        self.group_rows = round_up(-(-rows // (LANES // self.width)), 8)
        self.groups = -(-rows // self.group_rows)
        self.couple_at = [0, 0]
        for level in range(1, LEVELS):
            self.couple_at.append(self.couple_at[-1] + self.order[level])
        self.couple = self.couple_at[LEVELS]
        self.ancestors = [sum(self.order[:level]) for level in range(LEVELS + 1)]
        own = (LEVELS - 1) * sources
        at = self.couple
        self.rhs_at = at if at % LANES + own <= LANES else round_up(at, LANES)
        self.couple_wide = round_up(self.rhs_at + own, LANES)
        self.flips = [0, 2, 4, 6]

    def shared(self, level):
        return [flip for flip in self.flips if flip < self.members[level]]

    def open_bits(self, level):
        bits = range(self.members[level].bit_length() - 1)
        return [bit for bit in bits if (1 << bit) not in (2, 4)]

    def local(self, level):
        position = lax.axis_index("leaf") * (self.total // self.leafs) + lax.axis_index("sub")
        return position & (self.members[level] - 1)


def transposed(block, scratch):
    scratch[...] = jnp.zeros_like(scratch)
    scratch[0 : block.shape[0], 0 : block.shape[1]] = block
    return scratch[...].T


def start_kernel(plan, rhs, coupling, wire, joined, scratch):
    first = jnp.concatenate([rhs[0, 0], rhs[1, 0]], axis=0)
    first = transposed(first, scratch)
    padded = plan.groups * plan.group_rows
    blocks = [first[at : at + plan.group_rows] for at in range(0, padded, plan.group_rows)]
    packed = side_by_side(blocks, plan.width)
    wire[...] = jnp.broadcast_to(packed[None], wire.shape)
    whole = plan.couple // LANES * LANES
    tail = plan.couple - whole
    shift = plan.rhs_at % LANES
    for part in range(2):
        later = jnp.concatenate([rhs[part, level] for level in range(1, LEVELS)], axis=0)
        later = transposed(later, scratch)[0 : plan.rows]
        joined[part, :, 0:whole] = coupling[part, :, 0:whole]
        joined[part, :, plan.couple_wide - LANES :] = roll_right(later, shift)
        if tail:
            joined[part, :, whole : whole + tail] = coupling[part, :, whole : whole + tail]


def cut_kernel(plan, diag, middle):
    middle[...] = diag[:, :, plan.order[0] : sum(plan.order[:-1])]


def relay_kernel(plan, from_x, from_y, real, imag):
    real[...] = from_x[0]
    imag[...] = from_y[1]


def rhs_rows(plan, real, imag, level, shift_cols):
    start = plan.rhs_at // LANES * LANES - shift_cols
    offset = plan.rhs_at % LANES + plan.sources * (level - 1)
    re_part = roll_left(real[:, start : start + LANES], offset)
    im_part = roll_left(imag[:, start : start + LANES], offset - plan.sources)
    return jnp.where(lane_of(re_part.shape) < plan.sources, re_part, im_part)


def unpack_all(plan, near, far, target):
    g = plan.group_rows
    core = lax.axis_index("sub")
    for place, wires in ((core, near), (core ^ 1, far)):
        flat = wires[...].reshape(plan.leafs * g, LANES)
        for group in range(plan.groups):
            block = roll_left(flat, group * plan.width).reshape(plan.leafs, g, LANES)
            count = min(g, plan.rows - group * g)
            target[:, place, group * g : group * g + count, :] = block[:, 0:count]


def pack_all(plan, rows_block, wire):
    g = plan.group_rows
    padded = plan.groups * g
    if padded > plan.rows:
        extra = jnp.zeros((padded - plan.rows, LANES), jnp.float32)
        rows_block = jnp.concatenate([rows_block, extra], axis=0)
    blocks = [rows_block[at : at + g] for at in range(0, padded, g)]
    wire[...] = jnp.broadcast_to(side_by_side(blocks, plan.width)[None], wire.shape)


def top_kernel(plan, near, far, diag, wire, vector):
    unpack_all(plan, near, far, vector)
    packed = weights(vector[...].reshape(plan.order[0], LANES), plan.width)
    top = plan.order[0]
    pack_all(plan, product(diag[0, :, 0:top], diag[1, :, 0:top], packed, plan.width), wire)


def reduce_rows(plan, level, blocks, packed_first_col, packed):
    out = []
    first = plan.couple_at[level] - packed_first_col
    for real, imag in blocks:
        cols = slice(first, first + plan.order[level])
        value = product(real[:, cols], imag[:, cols], packed, plan.width)
        out.append(rhs_rows(plan, real, imag, level, packed_first_col) - value)
    return out


def first_reduce_kernel(
    plan, near, far, index, own, from_x, from_y, diag_re, diag_im, wire, top, rest, bounds
):
    unpack_all(plan, near, far, top)
    gather_rows(
        top.reshape(plan.order[0], LANES), index, plan.couple_at[1], plan.order[1], bounds
    )
    blocks = [
        (own.at[0], own.at[1]),
        (from_x.at[0], from_x.at[1]),
        (from_y.at[0], from_y.at[1]),
        (diag_re, diag_im),
    ]
    packed = weights(bounds[...], plan.width)
    wire[...] = side_by_side(reduce_rows(plan, 1, blocks, 0, packed), plan.width)
    for at, (real, imag) in enumerate(blocks):
        rest[at, 0] = real[:, plan.order[1] :]
        rest[at, 1] = imag[:, plan.order[1] :]


def first_solve_kernel(plan, flips, *refs):
    wires, refs = refs[: len(flips)], refs[len(flips) :]
    own, from_x, from_y, diag_re, diag_im, wire, rest, vector = refs
    order = plan.order[1]
    spread(wires, vector, 0, plan.local(1), flips, plan.shared(1), plan.rows, plan.width)
    packed = weights(vector[...], plan.width)
    blocks = [
        (own.at[0], own.at[1]),
        (from_x.at[0], from_x.at[1]),
        (from_y.at[0], from_y.at[1]),
        (diag_re, diag_im),
    ]
    solved = [product(re[:, 0:order], im[:, 0:order], packed, plan.width) for re, im in blocks]
    wire[...] = side_by_side(solved, plan.width)
    for at, (real, imag) in enumerate(blocks):
        rest[at, 0] = real[:, order:]
        rest[at, 1] = imag[:, order:]


def pack_owners(plan, row_map, local_rows, packing, out):
    slots = plan.rows * LEVELS // plan.leafs
    per_row = LANES // plan.width
    packing[...] = jnp.zeros_like(packing)

    def body(owner, carry):
        for slot in range(slots):
            row = row_map[0, owner * slots + slot]
            packing[slot % per_row, owner, pl.ds(slot // per_row, 1), :] = local_rows[
                pl.ds(row, 1), :
            ]
        return carry

    lax.fori_loop(0, plan.leafs, body, 0)
    lane = lane_of(out.shape)
    total = jnp.where(lane < plan.width, packing[0], 0.0)
    for at in range(1, per_row):
        inside = (lane >= at * plan.width) & (lane < (at + 1) * plan.width)
        total = jnp.where(inside, roll_right(packing[at], at * plan.width), total)
    out[...] = total


def own_rows(plan, vector, level):
    place = pl.multiple_of(plan.ancestors[level] + plan.local(level) * plan.rows, 8)
    return vector[pl.ds(place, plan.rows), :]


def last_diag(plan, diag):
    start = sum(plan.order[:-1])
    return diag[0, :, start:], diag[1, :, start:]


def tail_kernel(plan, flips, *refs):
    wires, refs = refs[: len(flips)], refs[len(flips) :]
    top, index, row_map, couple, couple_far, diag, diag_far, diag_own = refs[:8]
    out, vector, bounds, front, local_rows, packing = refs[8:]
    rows, width = plan.rows, plan.width
    vector[0 : plan.order[0], :] = top[...]
    spread(wires, vector, plan.order[0], plan.local(1), flips, plan.shared(1), rows, width)
    cut = plan.order[1]

    def held(level):
        found = []
        for at, flip in enumerate(plan.shared(level)):
            found.append((flip, couple.at[at], diag.at[at]))
            found.append((flip ^ 1, couple_far.at[at], diag_far.at[at]))
        return found

    for level in range(2, LEVELS):
        order = plan.order[level]
        local = plan.local(level)
        gather_rows(vector, index, plan.couple_at[level], order, bounds)
        packed = weights(bounds[0:order, :], width)
        blocks = [(pair.at[0], pair.at[1]) for _, pair, _ in held(level)]
        reduced = reduce_rows(plan, level, blocks, cut, packed)
        for (flip, _, _), value in zip(held(level), reduced):
            front[pl.ds(pl.multiple_of((local ^ flip) * rows, 8), rows), :] = value
        packed = weights(front[0:order, :], width)
        base = plan.ancestors[level]
        if level + 1 < LEVELS:
            for flip, _, pair in held(level):
                solved = product(pair[0], pair[1], packed, width)
                place = pl.multiple_of(base + (local ^ flip) * rows, 8)
                vector[pl.ds(place, rows), :] = solved
        else:
            local_rows[level * rows :, :] = product(*last_diag(plan, diag_own), packed, width)
    for level in range(LEVELS - 1):
        local_rows[level * rows : (level + 1) * rows, :] = own_rows(plan, vector, level)
    pack_owners(plan, row_map, local_rows, packing, out)


def reduce_kernel(plan, level, flips, *refs):
    wires, refs = refs[: len(flips)], refs[len(flips) :]
    top, index, couple, wire, vector, bounds = refs
    rows, width = plan.rows, plan.width
    vector[0 : plan.ancestors[level - 1], :] = top[...]
    spread(
        wires, vector, plan.ancestors[level - 1], plan.local(level - 1), flips,
        plan.shared(level - 1), rows, width,
    )
    gather_rows(vector, index, plan.couple_at[level], plan.order[level], bounds)
    blocks = [(couple.at[at, 0], couple.at[at, 1]) for at in range(len(plan.shared(level)))]
    packed = weights(bounds[...], width)
    wire[...] = side_by_side(reduce_rows(plan, level, blocks, plan.order[1], packed), width)


def solve_kernel(plan, level, flips, first_col, *refs):
    wires, refs = refs[: len(flips)], refs[len(flips) :]
    diag, wire, vector = refs
    spread(wires, vector, 0, plan.local(level), flips, plan.shared(level), plan.rows, plan.width)
    packed = weights(vector[...], plan.width)
    cols = slice(first_col, first_col + plan.order[level])
    solved = [
        product(diag[at, 0, :, cols], diag[at, 1, :, cols], packed, plan.width)
        for at in range(len(plan.shared(level)))
    ]
    wire[...] = side_by_side(solved, plan.width)


def last_kernel(plan, flips, *refs):
    wires, refs = refs[: len(flips)], refs[len(flips) :]
    top, row_map, diag_own, out, front, local_rows, packing = refs
    level = LEVELS - 1
    rows, width = plan.rows, plan.width
    spread(wires, front, 0, plan.local(level), flips, plan.shared(level), rows, width)
    packed = weights(front[...], width)
    local_rows[level * rows :, :] = product(*last_diag(plan, diag_own), packed, width)
    for upper in range(level):
        local_rows[upper * rows : (upper + 1) * rows, :] = own_rows(plan, top, upper)
    pack_owners(plan, row_map, local_rows, packing, out)


def owner_kernel(plan, received, out, scratch):
    slots = plan.rows * LEVELS // plan.leafs
    per_row = LANES // plan.width
    for slot in range(slots):
        block = roll_left(received[:, slot // per_row, :], slot % per_row * plan.width)
        scratch[pl.ds(slot, plan.leafs, stride=slots), :] = block
    out[...] = scratch[...].T[0 : plan.width]


def call(kernel, plan, outs, scratch, args, scalars=(), static=()):
    specs = []
    for at in range(len(args)):
        space = pltpu.SMEM if at in scalars else pltpu.VMEM
        specs.append(pl.BlockSpec(memory_space=space))
    shapes = [jax.ShapeDtypeStruct(shape, jnp.float32) for shape in outs]
    return pl.pallas_call(
        functools.partial(kernel, plan, *static),
        out_shape=shapes,
        in_specs=specs,
        out_specs=[pl.BlockSpec(memory_space=pltpu.VMEM)] * len(outs),
        scratch_shapes=[pltpu.VMEM(shape, jnp.float32) for shape in scratch],
        compiler_params=pltpu.CompilerParams(vmem_limit_bytes=16 << 20),
    )(*args)


def local(right_sides, diag_inverse, coupling, boundary, plane_map):
    total = lax.axis_size(AXES)
    leafs = lax.axis_size("leaf")
    sources, rows = right_sides.shape[2], right_sides.shape[3]
    plan = Plan(total, leafs, rows, sources)
    order = plan.order
    per_row = LANES // plan.width
    owner_rows = -(-(rows * LEVELS // leafs) // per_row)
    packing = (per_row, leafs, owner_rows, LANES)
    wire_shape = (leafs, plan.group_rows, LANES)
    whole_shape = (leafs, total // leafs, rows, LANES)
    block = (rows, LANES)

    def flip_to(array, flip):
        route = [(device, device ^ flip) for device in range(total)]
        return lax.ppermute(array, AXES, route)

    def exchange(wire, level):
        bits = plan.open_bits(level)
        flips = [0]
        for bit in bits:
            flips = flips + [flip ^ (1 << bit) for flip in flips]
        if len(bits) <= 2:
            return [wire] + [flip_to(wire, flip) for flip in flips[1:]], flips
        current = wire[None]
        for bit in bits:
            current = jnp.concatenate([current, flip_to(current, 1 << bit)], axis=0)
        return [current[at] for at in range(len(flips))], flips

    def to_all(wire):
        near = lax.all_to_all(wire, "leaf", 0, 0)
        return near, flip_to(near, 1)

    def neighbours(array):
        return array, flip_to(array, 2), flip_to(array, 4)

    def beyond(pieces):
        own, from_x, from_y = pieces
        real, imag = call(relay_kernel, plan, [own.shape[1:]] * 2, [], [from_x, from_y])
        real, imag = flip_to(real, 4), flip_to(imag, 2)
        return own, from_x, from_y, real, imag

    wire, joined = call(
        start_kernel, plan, [wire_shape, (2, rows, plan.couple_wide)], [(LANES, LANES)],
        [right_sides, coupling],
    )
    (diag_mid,) = call(cut_kernel, plan, [(2, rows, sum(order[1:-1]))], [], [diag_inverse])
    gathered = to_all(wire)
    couple = beyond(neighbours(joined))
    (wire,) = call(top_kernel, plan, [wire_shape], [whole_shape], [*gathered, diag_inverse])
    gathered = to_all(wire)
    diag = beyond(neighbours(diag_mid))
    wire, top, couple_rest = call(
        first_reduce_kernel, plan,
        [block, whole_shape, (4, 2, rows, plan.couple_wide - order[1])],
        [(order[1], LANES)],
        [*gathered, boundary, *couple], scalars=(2,),
    )
    top = top.reshape(order[0], LANES)
    wires, flips = exchange(wire, 1)
    wire, diag_rest = call(
        first_solve_kernel, plan, [block, (4, 2, rows, diag_mid.shape[2] - order[1])],
        [(order[1], LANES)], [*wires, *diag], static=(flips,),
    )
    wires, flips = exchange(wire, 1)
    if plan.members[2] <= 8:
        couple_far = flip_to(couple_rest, 1)
        diag_far = flip_to(diag_rest, 1)
        (packed,) = call(
            tail_kernel, plan, [(leafs, owner_rows, LANES)],
            [
                (plan.ancestors[LEVELS - 1], LANES), (order[2], LANES), (order[2], LANES),
                (LEVELS * rows, LANES), packing,
            ],
            [
                *wires, top, boundary, plane_map, couple_rest, couple_far, diag_rest, diag_far,
                diag_inverse,
            ],
            scalars=(len(flips) + 1, len(flips) + 2), static=(flips,),
        )
    else:
        first_col = 0
        for level in range(2, LEVELS):
            wire, top = call(
                reduce_kernel, plan, [block, (plan.ancestors[level], LANES)],
                [(order[level], LANES)],
                [*wires, top, boundary, couple_rest], scalars=(len(flips) + 1,),
                static=(level, flips),
            )
            wires, flips = exchange(wire, level)
            if level + 1 < LEVELS:
                (wire,) = call(
                    solve_kernel, plan, [block], [(order[level], LANES)],
                    [*wires, diag_rest], static=(level, flips, first_col),
                )
                first_col += order[level]
                wires, flips = exchange(wire, level)
        (packed,) = call(
            last_kernel, plan, [(leafs, owner_rows, LANES)],
            [(order[-1], LANES), (LEVELS * rows, LANES), packing],
            [*wires, top, plane_map, diag_inverse], scalars=(len(flips) + 1,), static=(flips,),
        )
    received = lax.all_to_all(packed, "leaf", 0, 0)
    (field,) = call(
        owner_kernel, plan, [(plan.width, LEVELS * rows)], [(LEVELS * rows, LANES)], [received]
    )
    return field.reshape(2, sources, LEVELS * rows)


def solution(mesh):
    in_specs = (
        P(None, None, None, AXES),
        P(None, AXES, None),
        P(None, AXES, None),
        P(AXES, None),
        P(AXES, None),
    )
    out_specs = P(None, None, AXES)
    return jax.shard_map(local, mesh=mesh, in_specs=in_specs, out_specs=out_specs, check_vma=False)
```

```python
import functools

import jax
import jax.numpy as jnp
from jax import lax
from jax.experimental import pallas as pl
from jax.experimental.pallas import tpu as pltpu
from jax.sharding import PartitionSpec as P


LEVELS = 4
LANES = 128
AXES = ("leaf", "sub")


def round_up(value, step):
    return -(-value // step) * step


def roll_left(block, shift):
    shift = shift % LANES
    return block if shift == 0 else pltpu.roll(block, LANES - shift, axis=block.ndim - 1)


def roll_right(block, shift):
    return roll_left(block, LANES - shift % LANES)


def lane_of(shape):
    return lax.broadcasted_iota(jnp.int32, shape, len(shape) - 1)


def split(matrix):
    high = matrix.astype(jnp.bfloat16)
    rest = matrix - high.astype(jnp.float32)
    mid = rest.astype(jnp.bfloat16)
    low = (rest - mid.astype(jnp.float32)).astype(jnp.bfloat16)
    return [high, mid, low]


def weights(vectors, width):
    vectors = jnp.where(lane_of(vectors.shape) < width, vectors, 0.0)
    high = vectors.astype(jnp.bfloat16).astype(jnp.float32)
    rest = vectors - high
    mid = rest.astype(jnp.bfloat16).astype(jnp.float32)
    low = rest - mid
    return (high + roll_right(mid, width) + roll_right(low, 2 * width)).astype(jnp.bfloat16)


def product(real, imag, packed, width):
    rows = real.shape[0]
    stacked = jnp.concatenate(split(real) + split(imag), axis=0)
    terms = jnp.dot(stacked, packed, preferred_element_type=jnp.float32)

    def total(first):
        part = terms[first * rows : (first + 1) * rows]
        part = part + terms[(first + 1) * rows : (first + 2) * rows]
        part = part + terms[(first + 2) * rows : (first + 3) * rows]
        return part + roll_left(part, width) + roll_left(part, 2 * width)

    by_real, by_imag = total(0), total(3)
    half = width // 2
    swapped = jnp.where(
        lane_of(by_imag.shape) < half, -roll_left(by_imag, half), roll_right(by_imag, half)
    )
    return by_real + swapped


def side_by_side(blocks, width):
    lane = lane_of(blocks[0].shape)
    packed = jnp.where(lane < width, blocks[0], 0.0)
    for at in range(1, len(blocks)):
        inside = (lane >= at * width) & (lane < (at + 1) * width)
        packed = jnp.where(inside, roll_right(blocks[at], at * width), packed)
    return packed


def gather_rows(source, index, first, count, target):
    step = 8

    def body(turn, carry):
        for inner in range(step):
            row = turn * step + inner
            target[pl.ds(row, 1), :] = source[pl.ds(index[0, first + row], 1), :]
        return carry

    lax.fori_loop(0, count // step, body, 0)


def spread(wires, target, base, local, flips, lanes_flips, rows, width):
    for entry, flip in enumerate(flips):
        wire = wires[entry][...]
        for lane_block, lane_flip in enumerate(lanes_flips):
            place = pl.multiple_of(base + (local ^ (flip ^ lane_flip)) * rows, 8)
            target[pl.ds(place, rows), :] = roll_left(wire, lane_block * width)


class Plan:
    def __init__(self, total, leafs, rows, sources):
        self.total, self.leafs, self.rows, self.sources = total, leafs, rows, sources
        self.width = 2 * sources
        self.members = [total >> level for level in range(LEVELS)]
        self.order = [members * rows for members in self.members]
        self.group_rows = round_up(-(-rows // (LANES // self.width)), 8)
        self.groups = -(-rows // self.group_rows)
        self.couple_at = [0, 0]
        for level in range(1, LEVELS):
            self.couple_at.append(self.couple_at[-1] + self.order[level])
        self.couple = self.couple_at[LEVELS]
        self.ancestors = [sum(self.order[:level]) for level in range(LEVELS + 1)]
        own = (LEVELS - 1) * sources
        at = self.couple
        self.rhs_at = at if at % LANES + own <= LANES else round_up(at, LANES)
        self.couple_wide = round_up(self.rhs_at + own, LANES)
        self.rest_couple = self.couple_wide - self.order[1]
        self.rest_wide = self.rest_couple + sum(self.order[2:-1])
        self.join_diag = self.order[1] + LANES
        self.join_wide = self.join_diag + self.order[1]
        self.couple_flips, self.diag_flips, self.flips = [0, 2, 1, 3], [0, 4, 1, 5], [0, 2, 4, 6]

    def shared(self, level):
        return [flip for flip in self.flips if flip < self.members[level]]

    def open_bits(self, level, shared):
        bits = range(self.members[level].bit_length() - 1)
        return [bit for bit in bits if (1 << bit) not in shared]

    def local(self, level):
        position = lax.axis_index("leaf") * (self.total // self.leafs) + lax.axis_index("sub")
        return position & (self.members[level] - 1)


def transposed(block, scratch):
    scratch[...] = jnp.zeros_like(scratch)
    scratch[0 : block.shape[0], 0 : block.shape[1]] = block
    return scratch[...].T


def start_kernel(plan, rhs, wire, late, scratch):
    first = jnp.concatenate([rhs[0, 0], rhs[1, 0]], axis=0)
    first = transposed(first, scratch)
    padded = plan.groups * plan.group_rows
    blocks = [first[at : at + plan.group_rows] for at in range(0, padded, plan.group_rows)]
    packed = side_by_side(blocks, plan.width)
    wire[...] = jnp.broadcast_to(packed[None], wire.shape)
    for part in range(2):
        later = jnp.concatenate([rhs[part, level] for level in range(1, LEVELS)], axis=0)
        late[part] = transposed(later, scratch)[0 : plan.rows]


def cut_kernel(plan, coupling, diag, late, couple, diag_first, rest):
    first = plan.order[1]
    whole = plan.couple // LANES * LANES
    tail = plan.couple - whole
    shift = plan.rhs_at % LANES
    for part in range(2):
        couple[part, :, 0:first] = coupling[part, :, 0:first]
        couple[part, :, first:] = late[part]
        diag_first[part] = diag[part, :, plan.order[0] : plan.order[0] + first]
        rest[part, :, 0 : whole - first] = coupling[part, :, first:whole]
        start = plan.rhs_at // LANES * LANES - first
        rest[part, :, start : start + LANES] = roll_right(late[part], shift)
        if tail:
            rest[part, :, whole - first : plan.couple - first] = coupling[part, :, whole:]
        rest[part, :, plan.rest_couple :] = diag[
            part, :, plan.order[0] + first : sum(plan.order[:-1])
        ]


def join_kernel(plan, couple, from_x, diag, from_y, joined):
    for at, (left, right) in enumerate(((couple, diag), (from_x, from_y))):
        joined[at, :, :, 0 : plan.join_diag] = left[...]
        joined[at, :, :, plan.join_diag :] = right[...]


def relay_kernel(plan, from_x, from_y, real, imag):
    real[...] = from_x[0]
    imag[...] = from_y[1]


def rest_join_kernel(plan, own, from_x, from_y, real, imag, held):
    held[0] = own[...]
    held[1] = from_x[...]
    held[2] = from_y[...]
    held[3, 0] = real[...]
    held[3, 1] = imag[...]


def rhs_rows(plan, real, imag, start, offset):
    re_part = roll_left(real[:, start : start + LANES], offset)
    im_part = roll_left(imag[:, start : start + LANES], offset - plan.sources)
    return jnp.where(lane_of(re_part.shape) < plan.sources, re_part, im_part)


def unpack_all(plan, near, far, target):
    g = plan.group_rows
    core = lax.axis_index("sub")
    for place, wires in ((core, near), (core ^ 1, far)):
        flat = wires[...].reshape(plan.leafs * g, LANES)
        for group in range(plan.groups):
            block = roll_left(flat, group * plan.width).reshape(plan.leafs, g, LANES)
            count = min(g, plan.rows - group * g)
            target[:, place, group * g : group * g + count, :] = block[:, 0:count]


def pack_all(plan, rows_block, wire):
    g = plan.group_rows
    padded = plan.groups * g
    if padded > plan.rows:
        extra = jnp.zeros((padded - plan.rows, LANES), jnp.float32)
        rows_block = jnp.concatenate([rows_block, extra], axis=0)
    blocks = [rows_block[at : at + g] for at in range(0, padded, g)]
    wire[...] = jnp.broadcast_to(side_by_side(blocks, plan.width)[None], wire.shape)


def top_kernel(plan, near, far, diag, wire, vector):
    unpack_all(plan, near, far, vector)
    packed = weights(vector[...].reshape(plan.order[0], LANES), plan.width)
    top = plan.order[0]
    pack_all(plan, product(diag[0, :, 0:top], diag[1, :, 0:top], packed, plan.width), wire)


def reduce_rows(plan, level, blocks, packed):
    first, start, offset = 0, plan.order[1], 0
    if level > 1:
        first = plan.couple_at[level] - plan.order[1]
        start = plan.rhs_at // LANES * LANES - plan.order[1]
        offset = plan.rhs_at % LANES + plan.sources * (level - 1)
    out = []
    for pair in blocks:
        real, imag = pair.at[0], pair.at[1]
        cols = slice(first, first + plan.order[level])
        value = product(real[:, cols], imag[:, cols], packed, plan.width)
        out.append(rhs_rows(plan, real, imag, start, offset) - value)
    return out


def pairs_of(near, far):
    return [near.at[0], near.at[1], far.at[0], far.at[1]]


def first_reduce_kernel(plan, near, far, index, joined, joined_far, wire, top, bounds):
    unpack_all(plan, near, far, top)
    gather_rows(
        top.reshape(plan.order[0], LANES), index, plan.couple_at[1], plan.order[1], bounds
    )
    packed = weights(bounds[...], plan.width)
    blocks = pairs_of(joined, joined_far)
    wire[...] = side_by_side(reduce_rows(plan, 1, blocks, packed), plan.width)


def first_solve_kernel(plan, flips, *refs):
    wires, refs = refs[: len(flips)], refs[len(flips) :]
    joined, joined_far, wire, vector = refs
    cols = slice(plan.join_diag, plan.join_wide)
    spread(wires, vector, 0, plan.local(1), flips, plan.couple_flips, plan.rows, plan.width)
    packed = weights(vector[...], plan.width)
    solved = []
    for pair in pairs_of(joined, joined_far):
        solved.append(product(pair[0, :, cols], pair[1, :, cols], packed, plan.width))
    wire[...] = side_by_side(solved, plan.width)


def pack_owners(plan, row_map, local_rows, packing, out):
    slots = plan.rows * LEVELS // plan.leafs
    per_row = LANES // plan.width
    packing[...] = jnp.zeros_like(packing)

    def body(owner, carry):
        for slot in range(slots):
            row = row_map[0, owner * slots + slot]
            packing[slot % per_row, owner, pl.ds(slot // per_row, 1), :] = local_rows[
                pl.ds(row, 1), :
            ]
        return carry

    lax.fori_loop(0, plan.leafs, body, 0)
    lane = lane_of(out.shape)
    total = jnp.where(lane < plan.width, packing[0], 0.0)
    for at in range(1, per_row):
        inside = (lane >= at * plan.width) & (lane < (at + 1) * plan.width)
        total = jnp.where(inside, roll_right(packing[at], at * plan.width), total)
    out[...] = total


def own_rows(plan, vector, level):
    place = pl.multiple_of(plan.ancestors[level] + plan.local(level) * plan.rows, 8)
    return vector[pl.ds(place, plan.rows), :]


def last_diag(plan, diag):
    start = sum(plan.order[:-1])
    return diag[0, :, start:], diag[1, :, start:]


def tail_kernel(plan, flips, *refs):
    wires, refs = refs[: len(flips)], refs[len(flips) :]
    top, index, row_map, near, far, diag_own = refs[:6]
    out, vector, bounds, front, local_rows, packing = refs[6:]
    rows, width = plan.rows, plan.width
    vector[0 : plan.order[0], :] = top[...]
    spread(wires, vector, plan.order[0], plan.local(1), flips, plan.diag_flips, rows, width)

    def held(level):
        found = []
        for at, flip in enumerate(plan.shared(level)):
            found.append((flip, near.at[at]))
            found.append((flip ^ 1, far.at[at]))
        return found

    for level in range(2, LEVELS):
        order = plan.order[level]
        local = plan.local(level)
        gather_rows(vector, index, plan.couple_at[level], order, bounds)
        packed = weights(bounds[0:order, :], width)
        reduced = reduce_rows(plan, level, [pair for _, pair in held(level)], packed)
        for (flip, _), value in zip(held(level), reduced):
            front[pl.ds(pl.multiple_of((local ^ flip) * rows, 8), rows), :] = value
        packed = weights(front[0:order, :], width)
        base = plan.ancestors[level]
        if level + 1 < LEVELS:
            start = plan.rest_couple + sum(plan.order[2:level])
            for flip, pair in held(level):
                cols = slice(start, start + order)
                solved = product(pair[0, :, cols], pair[1, :, cols], packed, width)
                place = pl.multiple_of(base + (local ^ flip) * rows, 8)
                vector[pl.ds(place, rows), :] = solved
        else:
            local_rows[level * rows :, :] = product(*last_diag(plan, diag_own), packed, width)
    for level in range(LEVELS - 1):
        local_rows[level * rows : (level + 1) * rows, :] = own_rows(plan, vector, level)
    pack_owners(plan, row_map, local_rows, packing, out)


def reduce_kernel(plan, level, flips, lane_flips, *refs):
    wires, refs = refs[: len(flips)], refs[len(flips) :]
    top, index, held, wire, vector, bounds = refs
    upper = plan.ancestors[level - 1]
    vector[0:upper, :] = top[...]
    spread(
        wires, vector, upper, plan.local(level - 1), flips, lane_flips, plan.rows, plan.width
    )
    gather_rows(vector, index, plan.couple_at[level], plan.order[level], bounds)
    blocks = [held.at[at] for at in range(len(plan.shared(level)))]
    packed = weights(bounds[...], plan.width)
    wire[...] = side_by_side(reduce_rows(plan, level, blocks, packed), plan.width)


def solve_kernel(plan, level, flips, *refs):
    wires, refs = refs[: len(flips)], refs[len(flips) :]
    held, wire, vector = refs
    spread(wires, vector, 0, plan.local(level), flips, plan.shared(level), plan.rows, plan.width)
    packed = weights(vector[...], plan.width)
    start = plan.rest_couple + sum(plan.order[2:level])
    cols = slice(start, start + plan.order[level])
    solved = []
    for at in range(len(plan.shared(level))):
        solved.append(product(held[at, 0, :, cols], held[at, 1, :, cols], packed, plan.width))
    wire[...] = side_by_side(solved, plan.width)


def last_kernel(plan, flips, *refs):
    wires, refs = refs[: len(flips)], refs[len(flips) :]
    top, row_map, diag_own, out, front, local_rows, packing = refs
    level = LEVELS - 1
    rows, width = plan.rows, plan.width
    spread(wires, front, 0, plan.local(level), flips, plan.shared(level), rows, width)
    packed = weights(front[...], width)
    local_rows[level * rows :, :] = product(*last_diag(plan, diag_own), packed, width)
    for upper in range(level):
        local_rows[upper * rows : (upper + 1) * rows, :] = own_rows(plan, top, upper)
    pack_owners(plan, row_map, local_rows, packing, out)


def owner_kernel(plan, received, out, scratch):
    slots = plan.rows * LEVELS // plan.leafs
    per_row = LANES // plan.width
    for slot in range(slots):
        block = roll_left(received[:, slot // per_row, :], slot % per_row * plan.width)
        scratch[pl.ds(slot, plan.leafs, stride=slots), :] = block
    out[...] = scratch[...].T[0 : plan.width]


def call(kernel, plan, outs, scratch, args, scalars=(), static=()):
    specs = []
    for at in range(len(args)):
        space = pltpu.SMEM if at in scalars else pltpu.VMEM
        specs.append(pl.BlockSpec(memory_space=space))
    shapes = [jax.ShapeDtypeStruct(shape, jnp.float32) for shape in outs]
    return pl.pallas_call(
        functools.partial(kernel, plan, *static),
        out_shape=shapes,
        in_specs=specs,
        out_specs=[pl.BlockSpec(memory_space=pltpu.VMEM)] * len(outs),
        scratch_shapes=[pltpu.VMEM(shape, jnp.float32) for shape in scratch],
        compiler_params=pltpu.CompilerParams(vmem_limit_bytes=16 << 20),
    )(*args)


def local(right_sides, diag_inverse, coupling, boundary, plane_map):
    total = lax.axis_size(AXES)
    leafs = lax.axis_size("leaf")
    sources, rows = right_sides.shape[2], right_sides.shape[3]
    plan = Plan(total, leafs, rows, sources)
    order = plan.order
    per_row = LANES // plan.width
    owner_rows = -(-(rows * LEVELS // leafs) // per_row)
    packing = (per_row, leafs, owner_rows, LANES)
    wire_shape = (leafs, plan.group_rows, LANES)
    whole_shape = (leafs, total // leafs, rows, LANES)
    block = (rows, LANES)

    def flip_to(array, flip):
        route = [(device, device ^ flip) for device in range(total)]
        return lax.ppermute(array, AXES, route)

    def exchange(wire, level, shared):
        bits = plan.open_bits(level, shared)
        flips = [0]
        for bit in bits:
            flips = flips + [flip ^ (1 << bit) for flip in flips]
        if len(bits) <= 2:
            return [wire] + [flip_to(wire, flip) for flip in flips[1:]], flips
        current = wire[None]
        for bit in bits:
            current = jnp.concatenate([current, flip_to(current, 1 << bit)], axis=0)
        return [current[at] for at in range(len(flips))], flips

    def to_all(wire):
        near = lax.all_to_all(wire, "leaf", 0, 0)
        return near, flip_to(near, 1)

    part = (2, rows)
    wire, late = call(
        start_kernel, plan, [wire_shape, (*part, LANES)], [(LANES, LANES)], [right_sides]
    )
    couple, diag_first, rest = call(
        cut_kernel, plan,
        [(*part, plan.join_diag), (*part, order[1]), (*part, plan.rest_wide)], [],
        [coupling, diag_inverse, late],
    )
    gathered = to_all(wire)
    from_x, from_y = flip_to(couple, 2), flip_to(diag_first, 4)
    (wire,) = call(top_kernel, plan, [wire_shape], [whole_shape], [*gathered, diag_inverse])
    gathered = to_all(wire)
    (joined,) = call(
        join_kernel, plan, [(2, *part, plan.join_wide)], [],
        [couple, from_x, diag_first, from_y],
    )
    joined_far = flip_to(joined, 1)
    rest_x, rest_y = flip_to(rest, 2), flip_to(rest, 4)
    wire, top = call(
        first_reduce_kernel, plan, [block, whole_shape], [(order[1], LANES)],
        [*gathered, boundary, joined, joined_far], scalars=(2,),
    )
    top = top.reshape(order[0], LANES)
    wires, flips = exchange(wire, 1, (1, 2))
    real, imag = call(relay_kernel, plan, [(rows, plan.rest_wide)] * 2, [], [rest_x, rest_y])
    real, imag = flip_to(real, 4), flip_to(imag, 2)
    (wire,) = call(
        first_solve_kernel, plan, [block], [(order[1], LANES)],
        [*wires, joined, joined_far], static=(flips,),
    )
    wires, flips = exchange(wire, 1, (1, 4))
    (held,) = call(
        rest_join_kernel, plan, [(4, *part, plan.rest_wide)], [],
        [rest, rest_x, rest_y, real, imag],
    )
    if plan.members[2] <= 8:
        held_far = flip_to(held, 1)
        (packed,) = call(
            tail_kernel, plan, [(leafs, owner_rows, LANES)],
            [
                (plan.ancestors[LEVELS - 1], LANES), (order[2], LANES), (order[2], LANES),
                (LEVELS * rows, LANES), packing,
            ],
            [*wires, top, boundary, plane_map, held, held_far, diag_inverse],
            scalars=(len(flips) + 1, len(flips) + 2), static=(flips,),
        )
    else:
        lane_flips = plan.diag_flips
        for level in range(2, LEVELS):
            wire, top = call(
                reduce_kernel, plan, [block, (plan.ancestors[level], LANES)],
                [(order[level], LANES)], [*wires, top, boundary, held],
                scalars=(len(flips) + 1,), static=(level, flips, lane_flips),
            )
            lane_flips = plan.shared(level)
            wires, flips = exchange(wire, level, (2, 4))
            if level + 1 < LEVELS:
                (wire,) = call(
                    solve_kernel, plan, [block], [(order[level], LANES)],
                    [*wires, held], static=(level, flips),
                )
                wires, flips = exchange(wire, level, (2, 4))
        (packed,) = call(
            last_kernel, plan, [(leafs, owner_rows, LANES)],
            [(order[-1], LANES), (LEVELS * rows, LANES), packing],
            [*wires, top, plane_map, diag_inverse], scalars=(len(flips) + 1,), static=(flips,),
        )
    received = lax.all_to_all(packed, "leaf", 0, 0)
    (field,) = call(
        owner_kernel, plan, [(plan.width, LEVELS * rows)], [(LEVELS * rows, LANES)], [received]
    )
    return field.reshape(2, sources, LEVELS * rows)


def solution(mesh):
    in_specs = (
        P(None, None, None, AXES),
        P(None, AXES, None),
        P(None, AXES, None),
        P(AXES, None),
        P(AXES, None),
    )
    out_specs = P(None, None, AXES)
    return jax.shard_map(local, mesh=mesh, in_specs=in_specs, out_specs=out_specs, check_vma=False)
```
